256 devices in a mesh: ep: 64 (over z, y, core), dp: 4 (over x).
Axes of the slice: x: 4, y: 4, z: 8, core: 2. Of those that a mesh axis runs over, the one named last changes fastest.
Arguments:
- master_weight: float32 [128, 3584, 128], P('ep', 'dp'), may hold values from -3 to 3
- first_moment: float32 [128, 3584, 128], P('ep', 'dp'), may hold values from -2 to 2
- second_moment: float32 [128, 3584, 128], P('ep', 'dp'), may hold values from 0.05 to 2
- grad_owned: bfloat16 [4, 128, 3584, 128], P('dp', 'ep'), may hold values from -2.5 to 2.5
- grad_replica: bfloat16 [4, 128, 3584, 128], P('dp', 'ep'), may hold values from -2.5 to 2.5
- old_experts: int32 [128], replicated, may hold values from 0 to 127, each once
- new_experts: int32 [128], replicated, may hold values from 0 to 127, each once
- rep_expert: int32 [128], replicated, may hold values from 0 to 127
- rep_count: int32 [64], replicated, may hold values from 0 to 2, as said below
Outputs:
- new_weight: float32 [128, 3584, 128], P('ep', 'dp')
- new_first: float32 [128, 3584, 128], P('ep', 'dp')
- new_second: float32 [128, 3584, 128], P('ep', 'dp')
The draws below stay inside these ranges and needn't reach their ends.
Inputs may be any that keep to these rules, and one draw needn't show every extreme that they name: `old_experts`: each expert appears once. `new_experts`: each expert appears once. The first rep_count[i] of the 2 replica slots of ep index i are live; some index has all live and some none.
All inputs are finite; a program needn't handle non-finite values.
Results may differ from the reference program's by a relative error of at most 0.0003.
Values may be sent and summed in bfloat16 or wider, within the bound.
A program may use at most 64 MiB of HBM per device.

```python
import math
import jax
import jax.numpy as jnp
import numpy as np
from jax import lax

D = 3584
SLAB = 128
REP_SLOTS = 2
EXPERTS = 128
RSLOTS = 128
N_EP = 64
N_DP = 4


def draw_rep_count(key, part):
    rolls = jax.random.randint(jax.random.fold_in(key, 11), (N_EP,), 0, 8)
    counts = (rolls >= 5).astype(jnp.int32) + (rolls >= 7).astype(jnp.int32)
    counts = jnp.minimum(counts, REP_SLOTS)
    first_full = jax.random.randint(jax.random.fold_in(key, 12), (), 0, N_EP)
    counts = counts.at[first_full].set(REP_SLOTS)
    counts = counts.at[(first_full + 1) % N_EP].set(0)
    return counts.astype(jnp.int32)


def plant(drawn, key, low, largest):
    longest = drawn.shape.index(max(drawn.shape))
    spots = []
    for shift in (0, 1):
        where = [jax.random.randint(jax.random.fold_in(key, axis), (), 0, length) for axis, length in enumerate(drawn.shape)]
        where[longest] = (where[longest] + shift) % drawn.shape[longest]
        spots.append(tuple(where))
    return drawn.at[spots[0]].set(low).at[spots[1]].set(largest)


def block_scale(own_key, extent, split, low, largest):
    gain, own = 1.0, jax.random.fold_in(own_key, 6)
    for position, shards_of in split:
        draws = jnp.exp(jax.random.uniform(jax.random.fold_in(own, position), (shards_of,), jnp.float32, low / len(split), largest / len(split)))
        gain = gain * jnp.repeat(draws, extent[position] // shards_of).reshape([-1 if axis == position else 1 for axis in range(len(extent))])
    return gain


def rank_bounds(amount, slope):
    weights = [(1 << 20) // math.isqrt(standing ** slope) + 1 for standing in range(1, amount + 1)]
    scale = 1 + sum(weights) // (1 << 30)
    return np.cumsum(np.array([max(1, weight // scale) for weight in weights]))


def ranked(key, shape, number_of, skew):
    grid = rank_bounds(number_of, skew)
    pick = jax.random.randint(jax.random.fold_in(key, 1), shape, 0, int(grid[number_of - 1]))
    standing = jnp.searchsorted(jnp.asarray(grid, jnp.int32), pick, side="right")
    return jax.random.permutation(jax.random.fold_in(key, 2), number_of)[standing].astype(jnp.int32)


def bell_draw(own_key, shape, scale, bound, pieces=(), held_as=jnp.bfloat16):
    result = jax.random.normal(own_key, shape, jnp.float32) * scale
    if len(pieces) > 0:
        result = block_scale(own_key, shape, pieces, -0.22, 0.18) * result
    return jnp.clip(result, min=-bound, max=bound).astype(held_as)


def setup_inputs(seed: int = 0) -> dict:
    splits = jax.random.split(jax.random.key(seed), 10)
    master_weight = bell_draw(splits[0], (EXPERTS, D, SLAB), 0.5, 3.0, ((0, 64), (1, 4)), jnp.float32)
    first_moment = bell_draw(splits[1], (EXPERTS, D, SLAB), 0.3, 2.0, ((0, 64), (1, 4)), jnp.float32)
    second_moment = jnp.clip(jnp.exp(math.log(2.0) - 3.6888794 * jax.random.uniform(splits[2], (EXPERTS, D, SLAB), jnp.float32) ** block_scale(splits[2], (EXPERTS, D, SLAB), ((0, 64), (1, 4)), -0.2, 0.2)), 0.05, 2.0)
    grad_owned = bell_draw(splits[3], (N_DP, EXPERTS, D, SLAB), 0.3, 2.5, ((0, 4), (1, 64)))
    grad_replica = bell_draw(splits[4], (N_DP, RSLOTS, D, SLAB), 0.3, 2.5, ((0, 4), (1, 64)))
    old_experts = jax.random.permutation(splits[5], EXPERTS).astype(jnp.int32)
    new_experts = jax.random.permutation(splits[6], EXPERTS).astype(jnp.int32)
    rep_expert = plant(ranked(splits[7], (RSLOTS,), EXPERTS, 2), jax.random.fold_in(splits[7], 3), 0, EXPERTS - 1).astype(jnp.int32)
    rep_count = draw_rep_count(jax.random.fold_in(splits[9], 71), 0)
    return {"master_weight": master_weight, "first_moment": first_moment, "second_moment": second_moment, "grad_owned": grad_owned, "grad_replica": grad_replica, "old_experts": old_experts, "new_experts": new_experts, "rep_expert": rep_expert, "rep_count": rep_count}


beta_first = 0.9
beta_second = 0.95
learn_rate = 0.01
decay_rate = 0.1
adam_eps = 1e-08
corr_first = 1.0 - 0.9 ** 10
corr_second = 1.0 - 0.95 ** 10

def reference(master_weight, first_moment, second_moment, grad_owned, grad_replica, old_experts, new_experts, rep_expert, rep_count):
    owned = lax.optimization_barrier(jnp.sum(grad_owned.astype(jnp.float32), axis=0))
    live_mask = (jnp.arange(RSLOTS, dtype=jnp.int32) % REP_SLOTS < jnp.repeat(rep_count, REP_SLOTS)).astype(jnp.float32)
    replicas = lax.optimization_barrier(jnp.sum(grad_replica.astype(jnp.float32), axis=0))
    replica_match = jnp.where(rep_expert[None, :] == old_experts[:, None], live_mask[None, :], jnp.float32(0.0))
    gradient = owned + jnp.einsum('qs,sdc->qdc', replica_match, replicas, precision=lax.Precision.HIGHEST)
    moved_first = beta_first * first_moment + (1.0 - beta_first) * gradient
    moved_second = beta_second * second_moment + (1.0 - beta_second) * gradient * gradient
    step_size = moved_first / corr_first / (jnp.sqrt(moved_second / corr_second) + adam_eps)
    moved_weight = master_weight - learn_rate * (step_size + decay_rate * master_weight)
    source_index = lax.optimization_barrier(jnp.sum(jnp.where(new_experts[:, None] == old_experts[None, :], jnp.arange(EXPERTS, dtype=jnp.int32)[None, :], 0), axis=1)).astype(jnp.int32)
    return (jnp.take(moved_weight, source_index, axis=0), jnp.take(moved_first, source_index, axis=0), jnp.take(moved_second, source_index, axis=0))
```

```python
import jax
import jax.numpy as jnp
from jax import lax
from jax.sharding import PartitionSpec as P

beta_first = 0.9
beta_second = 0.95
learn_rate = 0.01
decay_rate = 0.1
adam_eps = 1e-08
corr_first = 1.0 - 0.9**10
corr_second = 1.0 - 0.95**10


def adam_update(weight_now, first_now, second_now, gradient):
    moved_first = beta_first * first_now + (1.0 - beta_first) * gradient
    moved_second = beta_second * second_now + (1.0 - beta_second) * gradient * gradient
    step_size = moved_first / corr_first / (jnp.sqrt(moved_second / corr_second) + adam_eps)
    moved_weight = weight_now - learn_rate * (step_size + decay_rate * weight_now)
    return (moved_weight, moved_first, moved_second)


def per_device(
    master_weight,
    first_moment,
    second_moment,
    grad_owned,
    grad_replica,
    old_experts,
    new_experts,
    rep_expert,
    rep_count,
):
    ep_count = lax.axis_size("ep")
    exp_dev, shard_rows, columns = master_weight.shape
    rep_dev = grad_replica.shape[1]
    piece_rows = shard_rows // ep_count
    experts = exp_dev * ep_count
    replica_slots = rep_dev * ep_count

    state = jnp.stack([master_weight, first_moment, second_moment])
    state_p = lax.all_to_all(
        state.reshape(3, exp_dev, ep_count, piece_rows, columns),
        "ep",
        split_axis=2,
        concat_axis=1,
        tiled=True,
    ).reshape(3, experts, piece_rows, columns)

    owned_part = lax.psum_scatter(
        grad_owned[0].astype(jnp.float32), "dp", scatter_dimension=1, tiled=True
    )
    replica_part = lax.psum_scatter(
        grad_replica[0].astype(jnp.float32), "dp", scatter_dimension=1, tiled=True
    )
    grads = jnp.concatenate([owned_part, replica_part], axis=0)
    grads_p = lax.all_to_all(
        grads.reshape(exp_dev + rep_dev, ep_count, piece_rows, columns),
        "ep",
        split_axis=1,
        concat_axis=0,
        tiled=True,
    ).reshape(ep_count, exp_dev + rep_dev, piece_rows, columns)
    owned_t = grads_p[:, :exp_dev].reshape(experts, piece_rows, columns)
    replica_t = grads_p[:, exp_dev:].reshape(replica_slots, piece_rows * columns)

    live_mask = (
        lax.iota(jnp.int32, replica_slots) % rep_dev
        < jnp.repeat(rep_count, rep_dev, total_repeat_length=replica_slots)
    ).astype(jnp.float32)
    replica_match = jnp.where(
        rep_expert[None, :] == old_experts[:, None], live_mask[None, :], jnp.float32(0.0)
    )
    gradient = owned_t + jnp.dot(
        replica_match,
        replica_t,
        precision=lax.Precision.HIGHEST,
        preferred_element_type=jnp.float32,
    ).reshape(experts, piece_rows, columns)
    source_index = jnp.sum(
        jnp.where(
            new_experts[:, None] == old_experts[None, :], lax.iota(jnp.int32, experts)[None, :], 0
        ),
        axis=1,
    )
    moved = adam_update(state_p[0], state_p[1], state_p[2], gradient)
    moved = jnp.take(jnp.stack(moved), source_index, axis=1)
    back = lax.all_to_all(
        moved.reshape(3, ep_count, exp_dev, 1, piece_rows, columns),
        "ep",
        split_axis=1,
        concat_axis=3,
        tiled=True,
    ).reshape(3, exp_dev, shard_rows, columns)
    return (back[0], back[1], back[2])


def solution(mesh):
    in_specs = (
        P("ep", "dp", None),
        P("ep", "dp", None),
        P("ep", "dp", None),
        P("dp", "ep", None, None),
        P("dp", "ep", None, None),
        P(),
        P(),
        P(),
        P(),
    )
    out_specs = (P("ep", "dp", None), P("ep", "dp", None), P("ep", "dp", None))
    return jax.shard_map(
        per_device, mesh=mesh, in_specs=in_specs, out_specs=out_specs, check_vma=False
    )
```

```python
import jax
import jax.numpy as jnp
from jax import lax
from jax.sharding import PartitionSpec as P

beta_first = 0.9
beta_second = 0.95
learn_rate = 0.01
decay_rate = 0.1
adam_eps = 1e-08
corr_first = 1.0 - 0.9**10
corr_second = 1.0 - 0.95**10


def adam_update(weight_now, first_now, second_now, gradient):
    moved_first = beta_first * first_now + (1.0 - beta_first) * gradient
    moved_second = beta_second * second_now + (1.0 - beta_second) * gradient * gradient
    step_size = moved_first / corr_first / (jnp.sqrt(moved_second / corr_second) + adam_eps)
    moved_weight = weight_now - learn_rate * (step_size + decay_rate * weight_now)
    return (moved_weight, moved_first, moved_second)


def per_device_body(
    master_weight,
    first_moment,
    second_moment,
    grad_owned,
    grad_replica,
    old_experts,
    new_experts,
    rep_expert,
    rep_count,
):
    ep_count = lax.axis_size("ep")
    exp_dev, shard_rows, columns = master_weight.shape
    rep_dev = grad_replica.shape[1]
    piece_rows = shard_rows // ep_count
    experts = exp_dev * ep_count
    replica_slots = rep_dev * ep_count

    state = jnp.stack([master_weight, first_moment, second_moment])
    state_p = lax.all_to_all(
        state.reshape(3, exp_dev, ep_count, piece_rows, columns),
        "ep",
        split_axis=2,
        concat_axis=1,
        tiled=True,
    ).reshape(3, experts, piece_rows, columns)

    dp_count = lax.axis_size("dp")
    dp_index = lax.axis_index("dp")
    raw = jnp.concatenate([grad_owned[0], grad_replica[0]], axis=0).reshape(
        exp_dev + rep_dev, dp_count, shard_rows, columns
    )
    grads = lax.dynamic_index_in_dim(raw, dp_index, axis=1, keepdims=False).astype(jnp.float32)
    for shift in range(1, dp_count):
        block = lax.dynamic_index_in_dim(raw, (dp_index + shift) % dp_count, axis=1, keepdims=False)
        got = lax.ppermute(
            block, "dp", [(i, (i + shift) % dp_count) for i in range(dp_count)]
        )
        grads = grads + got.astype(jnp.float32)
    grads_p = lax.all_to_all(
        grads.reshape(exp_dev + rep_dev, ep_count, piece_rows, columns),
        "ep",
        split_axis=1,
        concat_axis=0,
        tiled=True,
    ).reshape(ep_count, exp_dev + rep_dev, piece_rows, columns)
    owned_t = grads_p[:, :exp_dev].reshape(experts, piece_rows, columns)
    replica_t = grads_p[:, exp_dev:].reshape(replica_slots, piece_rows * columns)

    live_mask = (
        lax.iota(jnp.int32, replica_slots) % rep_dev
        < jnp.repeat(rep_count, rep_dev, total_repeat_length=replica_slots)
    ).astype(jnp.float32)
    replica_match = jnp.where(
        rep_expert[None, :] == old_experts[:, None], live_mask[None, :], jnp.float32(0.0)
    )
    gradient = owned_t + jnp.dot(
        replica_match,
        replica_t,
        precision=lax.Precision.HIGHEST,
        preferred_element_type=jnp.float32,
    ).reshape(experts, piece_rows, columns)
    source_index = jnp.sum(
        jnp.where(
            new_experts[:, None] == old_experts[None, :], lax.iota(jnp.int32, experts)[None, :], 0
        ),
        axis=1,
    )
    moved = adam_update(state_p[0], state_p[1], state_p[2], gradient)
    moved = jnp.take(jnp.stack(moved), source_index, axis=1)
    back = lax.all_to_all(
        moved.reshape(3, ep_count, exp_dev, 1, piece_rows, columns),
        "ep",
        split_axis=1,
        concat_axis=3,
        tiled=True,
    ).reshape(3, exp_dev, shard_rows, columns)
    return (back[0], back[1], back[2])


def solution(mesh):
    in_specs = (
        P("ep", "dp", None),
        P("ep", "dp", None),
        P("ep", "dp", None),
        P("dp", "ep", None, None),
        P("dp", "ep", None, None),
        P(),
        P(),
        P(),
        P(),
    )
    out_specs = (P("ep", "dp", None), P("ep", "dp", None), P("ep", "dp", None))
    return jax.shard_map(
        per_device_body, mesh=mesh, in_specs=in_specs, out_specs=out_specs, check_vma=False
    )
```

```python
import jax
import jax.numpy as jnp
from jax import lax
from jax.sharding import PartitionSpec as P

beta_first = 0.9
beta_second = 0.95
learn_rate = 0.01
decay_rate = 0.1
adam_eps = 1e-08
corr_first = 1.0 - 0.9**10
corr_second = 1.0 - 0.95**10


def adam_update(weight_now, first_now, second_now, gradient):
    moved_first = beta_first * first_now + (1.0 - beta_first) * gradient
    moved_second = beta_second * second_now + (1.0 - beta_second) * gradient * gradient
    step_size = moved_first / corr_first / (jnp.sqrt(moved_second / corr_second) + adam_eps)
    moved_weight = weight_now - learn_rate * (step_size + decay_rate * weight_now)
    return (moved_weight, moved_first, moved_second)


def per_device_body(
    master_weight,
    first_moment,
    second_moment,
    grad_owned,
    grad_replica,
    old_experts,
    new_experts,
    rep_expert,
    rep_count,
):
    ep_count = lax.axis_size("ep")
    exp_dev, shard_rows, columns = master_weight.shape
    rep_dev = grad_replica.shape[1]
    piece_rows = shard_rows // ep_count
    experts = exp_dev * ep_count
    replica_slots = rep_dev * ep_count

    state = jnp.stack([master_weight, first_moment, second_moment])
    state_p = lax.all_to_all(
        state.reshape(3, exp_dev, ep_count, piece_rows, columns),
        "ep",
        split_axis=2,
        concat_axis=1,
        tiled=True,
    ).reshape(3, experts, piece_rows, columns)

    dp_count = lax.axis_size("dp")
    dp_index = lax.axis_index("dp")
    raw = jnp.concatenate([grad_owned[0], grad_replica[0]], axis=0).reshape(
        exp_dev + rep_dev, dp_count, shard_rows, columns
    )
    grads = lax.dynamic_index_in_dim(raw, dp_index, axis=1, keepdims=False).astype(jnp.float32)
    for shift in range(1, dp_count):
        block = lax.dynamic_index_in_dim(raw, (dp_index + shift) % dp_count, axis=1, keepdims=False)
        got = lax.ppermute(
            block, "dp", [(i, (i + shift) % dp_count) for i in range(dp_count)]
        )
        grads = grads + got.astype(jnp.float32)
    source_index = jnp.sum(
        jnp.where(
            new_experts[:, None] == old_experts[None, :], lax.iota(jnp.int32, experts)[None, :], 0
        ),
        axis=1,
    )
    state_new = jnp.take(state_p, source_index, axis=1)

    grads_p = lax.all_to_all(
        grads.reshape(exp_dev + rep_dev, ep_count, piece_rows, columns),
        "ep",
        split_axis=1,
        concat_axis=0,
        tiled=True,
    ).reshape(ep_count * (exp_dev + rep_dev), piece_rows * columns)

    column = lax.iota(jnp.int32, ep_count * (exp_dev + rep_dev))
    device_of, within = column // (exp_dev + rep_dev), column % (exp_dev + rep_dev)
    is_owned = within < exp_dev
    old_slot = jnp.clip(device_of * exp_dev + within, 0, experts - 1)
    rep_slot = jnp.clip(device_of * rep_dev + within - exp_dev, 0, replica_slots - 1)
    live = (rep_slot % rep_dev < rep_count[rep_slot // rep_dev]).astype(jnp.float32)
    column_expert = jnp.where(is_owned, old_experts[old_slot], rep_expert[rep_slot])
    column_weight = jnp.where(is_owned, jnp.float32(1.0), live)
    combine = jnp.where(
        new_experts[:, None] == column_expert[None, :], column_weight[None, :], jnp.float32(0.0)
    )
    gradient = jnp.dot(
        combine,
        grads_p,
        precision=lax.Precision.HIGHEST,
        preferred_element_type=jnp.float32,
    ).reshape(experts, piece_rows, columns)
    moved = jnp.stack(adam_update(state_new[0], state_new[1], state_new[2], gradient))
    back = lax.all_to_all(
        moved.reshape(3, ep_count, exp_dev, 1, piece_rows, columns),
        "ep",
        split_axis=1,
        concat_axis=3,
        tiled=True,
    ).reshape(3, exp_dev, shard_rows, columns)
    return (back[0], back[1], back[2])


def solution(mesh):
    in_specs = (
        P("ep", "dp", None),
        P("ep", "dp", None),
        P("ep", "dp", None),
        P("dp", "ep", None, None),
        P("dp", "ep", None, None),
        P(),
        P(),
        P(),
        P(),
    )
    out_specs = (P("ep", "dp", None), P("ep", "dp", None), P("ep", "dp", None))
    return jax.shard_map(
        per_device_body, mesh=mesh, in_specs=in_specs, out_specs=out_specs, check_vma=False
    )
```

```python
import jax
import jax.numpy as jnp
from jax import lax
from jax.sharding import PartitionSpec as P

beta_first = 0.9
beta_second = 0.95
learn_rate = 0.01
decay_rate = 0.1
adam_eps = 1e-08
corr_first = 1.0 - 0.9**10
corr_second = 1.0 - 0.95**10


def adam_update(weight_now, first_now, second_now, gradient):
    moved_first = beta_first * first_now + (1.0 - beta_first) * gradient
    moved_second = beta_second * second_now + (1.0 - beta_second) * gradient * gradient
    step_size = moved_first / corr_first / (jnp.sqrt(moved_second / corr_second) + adam_eps)
    moved_weight = weight_now - learn_rate * (step_size + decay_rate * weight_now)
    return (moved_weight, moved_first, moved_second)


def per_device_body(
    master_weight,
    first_moment,
    second_moment,
    grad_owned,
    grad_replica,
    old_experts,
    new_experts,
    rep_expert,
    rep_count,
):
    ep_count = lax.axis_size("ep")
    exp_dev, shard_rows, columns = master_weight.shape
    rep_dev = grad_replica.shape[1]
    piece_rows = shard_rows // ep_count
    experts = exp_dev * ep_count
    replica_slots = rep_dev * ep_count

    state = jnp.stack([master_weight, first_moment, second_moment])
    state_p = lax.all_to_all(
        state.reshape(3, exp_dev, ep_count, piece_rows, columns),
        "ep",
        split_axis=2,
        concat_axis=1,
        tiled=True,
    ).reshape(3, experts, piece_rows, columns)

    dp_count = lax.axis_size("dp")
    dp_index = lax.axis_index("dp")
    raw = jnp.concatenate([grad_owned[0], grad_replica[0]], axis=0).reshape(
        exp_dev + rep_dev, dp_count, shard_rows, columns
    )
    own_block = lax.dynamic_index_in_dim(raw, dp_index, axis=1, keepdims=False)
    received = []
    for shift in range(1, dp_count):
        block = lax.dynamic_index_in_dim(raw, (dp_index + shift) % dp_count, axis=1, keepdims=False)
        got = lax.ppermute(
            block, "dp", [(i, (i + shift) % dp_count) for i in range(dp_count)]
        )
        received.append(got)
    grads = own_block.astype(jnp.float32)
    for got in received:
        grads = grads + got.astype(jnp.float32)
    source_index = jnp.sum(
        jnp.where(
            new_experts[:, None] == old_experts[None, :], lax.iota(jnp.int32, experts)[None, :], 0
        ),
        axis=1,
    )
    state_new = jnp.take(state_p, source_index, axis=1)

    grads_p = lax.all_to_all(
        grads.reshape(exp_dev + rep_dev, ep_count, piece_rows, columns),
        "ep",
        split_axis=1,
        concat_axis=0,
        tiled=True,
    )
    grads_p = grads_p.reshape(ep_count * (exp_dev + rep_dev), piece_rows * columns)

    column = lax.iota(jnp.int32, ep_count * (exp_dev + rep_dev))
    device_of, within = column // (exp_dev + rep_dev), column % (exp_dev + rep_dev)
    is_owned = within < exp_dev
    old_slot = jnp.clip(device_of * exp_dev + within, 0, experts - 1)
    rep_slot = jnp.clip(device_of * rep_dev + within - exp_dev, 0, replica_slots - 1)
    live = (rep_slot % rep_dev < rep_count[rep_slot // rep_dev]).astype(jnp.float32)
    column_expert = jnp.where(is_owned, old_experts[old_slot], rep_expert[rep_slot])
    column_weight = jnp.where(is_owned, jnp.float32(1.0), live)
    combine = jnp.where(
        new_experts[:, None] == column_expert[None, :], column_weight[None, :], jnp.float32(0.0)
    )
    gradient = jnp.dot(
        combine,
        grads_p,
        precision=lax.Precision.HIGHEST,
        preferred_element_type=jnp.float32,
    ).reshape(experts, piece_rows, columns)
    moved = jnp.stack(adam_update(state_new[0], state_new[1], state_new[2], gradient))
    back = lax.all_to_all(
        moved.reshape(3, ep_count, exp_dev, 1, piece_rows, columns),
        "ep",
        split_axis=1,
        concat_axis=3,
        tiled=True,
    ).reshape(3, exp_dev, shard_rows, columns)
    return (back[0], back[1], back[2])


def solution(mesh):
    in_specs = (
        P("ep", "dp", None),
        P("ep", "dp", None),
        P("ep", "dp", None),
        P("dp", "ep", None, None),
        P("dp", "ep", None, None),
        P(),
        P(),
        P(),
        P(),
    )
    out_specs = (P("ep", "dp", None), P("ep", "dp", None), P("ep", "dp", None))
    return jax.shard_map(
        per_device_body, mesh=mesh, in_specs=in_specs, out_specs=out_specs, check_vma=False
    )
```

```python
import jax
import jax.numpy as jnp
from jax import lax
from jax.sharding import PartitionSpec as P

beta_first = 0.9
beta_second = 0.95
learn_rate = 0.01
decay_rate = 0.1
adam_eps = 1e-08
corr_first = 1.0 - 0.9**10
corr_second = 1.0 - 0.95**10


def adam_update(weight_now, first_now, second_now, gradient):
    moved_first = beta_first * first_now + (1.0 - beta_first) * gradient
    moved_second = beta_second * second_now + (1.0 - beta_second) * gradient * gradient
    step_size = moved_first / corr_first / (jnp.sqrt(moved_second / corr_second) + adam_eps)
    moved_weight = weight_now - learn_rate * (step_size + decay_rate * weight_now)
    return (moved_weight, moved_first, moved_second)


def per_device_body(
    master_weight,
    first_moment,
    second_moment,
    grad_owned,
    grad_replica,
    old_experts,
    new_experts,
    rep_expert,
    rep_count,
):
    ep_count = lax.axis_size("ep")
    exp_dev, shard_rows, columns = master_weight.shape
    rep_dev = grad_replica.shape[1]
    piece_rows = shard_rows // ep_count
    experts = exp_dev * ep_count
    replica_slots = rep_dev * ep_count

    state = jnp.stack([master_weight, first_moment, second_moment]).reshape(
        3, exp_dev, ep_count, piece_rows, columns
    )
    state_p = lax.all_to_all(
        state.transpose(2, 0, 1, 3, 4), "ep", split_axis=0, concat_axis=0, tiled=True
    )
    state_p = state_p.transpose(1, 0, 2, 3, 4).reshape(3, experts, piece_rows, columns)

    dp_count = lax.axis_size("dp")
    dp_index = lax.axis_index("dp")
    raw = jnp.concatenate([grad_owned[0], grad_replica[0]], axis=0).reshape(
        exp_dev + rep_dev, dp_count, shard_rows, columns
    )
    own_block = lax.dynamic_index_in_dim(raw, dp_index, axis=1, keepdims=False)
    received = []
    for shift in range(1, dp_count):
        block = lax.dynamic_index_in_dim(raw, (dp_index + shift) % dp_count, axis=1, keepdims=False)
        got = lax.ppermute(
            block, "dp", [(i, (i + shift) % dp_count) for i in range(dp_count)]
        )
        received.append(got)
    grads = own_block.astype(jnp.float32)
    for got in received:
        grads = grads + got.astype(jnp.float32)
    source_index = jnp.sum(
        jnp.where(
            new_experts[:, None] == old_experts[None, :], lax.iota(jnp.int32, experts)[None, :], 0
        ),
        axis=1,
    )
    state_new = jnp.take(state_p, source_index, axis=1)

    grads_p = lax.all_to_all(
        grads.reshape(exp_dev + rep_dev, ep_count, piece_rows, columns).transpose(1, 0, 2, 3),
        "ep",
        split_axis=0,
        concat_axis=0,
        tiled=True,
    )
    grads_p = grads_p.reshape(ep_count * (exp_dev + rep_dev), piece_rows * columns)

    column = lax.iota(jnp.int32, ep_count * (exp_dev + rep_dev))
    device_of, within = column // (exp_dev + rep_dev), column % (exp_dev + rep_dev)
    is_owned = within < exp_dev
    old_slot = jnp.clip(device_of * exp_dev + within, 0, experts - 1)
    rep_slot = jnp.clip(device_of * rep_dev + within - exp_dev, 0, replica_slots - 1)
    live = (rep_slot % rep_dev < rep_count[rep_slot // rep_dev]).astype(jnp.float32)
    column_expert = jnp.where(is_owned, old_experts[old_slot], rep_expert[rep_slot])
    column_weight = jnp.where(is_owned, jnp.float32(1.0), live)
    combine = jnp.where(
        new_experts[:, None] == column_expert[None, :], column_weight[None, :], jnp.float32(0.0)
    )
    gradient = jnp.dot(
        combine,
        grads_p,
        precision=lax.Precision.HIGHEST,
        preferred_element_type=jnp.float32,
    ).reshape(experts, piece_rows, columns)
    moved = jnp.stack(adam_update(state_new[0], state_new[1], state_new[2], gradient))
    back = lax.all_to_all(
        moved.reshape(3, ep_count, exp_dev, piece_rows, columns).transpose(1, 0, 2, 3, 4),
        "ep",
        split_axis=0,
        concat_axis=0,
        tiled=True,
    )
    back = back.transpose(1, 2, 0, 3, 4).reshape(3, exp_dev, shard_rows, columns)
    return (back[0], back[1], back[2])


def solution(mesh):
    in_specs = (
        P("ep", "dp", None),
        P("ep", "dp", None),
        P("ep", "dp", None),
        P("dp", "ep", None, None),
        P("dp", "ep", None, None),
        P(),
        P(),
        P(),
        P(),
    )
    out_specs = (P("ep", "dp", None), P("ep", "dp", None), P("ep", "dp", None))
    return jax.shard_map(
        per_device_body, mesh=mesh, in_specs=in_specs, out_specs=out_specs, check_vma=False
    )
```

```python
import jax
import jax.numpy as jnp
from jax import lax
from jax.sharding import PartitionSpec as P

beta_first = 0.9
beta_second = 0.95
learn_rate = 0.01
decay_rate = 0.1
adam_eps = 1e-08
corr_first = 1.0 - 0.9**10
corr_second = 1.0 - 0.95**10


def adam_update(weight_now, first_now, second_now, gradient):
    moved_first = beta_first * first_now + (1.0 - beta_first) * gradient
    moved_second = beta_second * second_now + (1.0 - beta_second) * gradient * gradient
    step_size = moved_first / corr_first / (jnp.sqrt(moved_second / corr_second) + adam_eps)
    moved_weight = weight_now - learn_rate * (step_size + decay_rate * weight_now)
    return (moved_weight, moved_first, moved_second)


def per_device_body(
    master_weight,
    first_moment,
    second_moment,
    grad_owned,
    grad_replica,
    old_experts,
    new_experts,
    rep_expert,
    rep_count,
):
    ep_count = lax.axis_size("ep")
    exp_dev, shard_rows, columns = master_weight.shape
    rep_dev = grad_replica.shape[1]
    piece_rows = shard_rows // ep_count
    experts = exp_dev * ep_count
    replica_slots = rep_dev * ep_count

    state = jnp.stack([master_weight, first_moment, second_moment]).reshape(
        3, exp_dev, ep_count, piece_rows, columns
    )
    state_p = lax.all_to_all(
        state.transpose(2, 0, 1, 3, 4), "ep", split_axis=0, concat_axis=0, tiled=True
    )
    state_p = state_p.transpose(1, 0, 2, 3, 4).reshape(3, experts, piece_rows, columns)

    dp_count = lax.axis_size("dp")
    dp_index = lax.axis_index("dp")
    def block_of(array, index):
        return lax.dynamic_slice_in_dim(array, index * shard_rows, shard_rows, axis=1)

    own_block = [block_of(grad_owned[0], dp_index), block_of(grad_replica[0], dp_index)]
    received = []
    for shift in range(1, dp_count):
        target = (dp_index + shift) % dp_count
        received.append(
            [
                lax.ppermute(
                    block_of(array, target),
                    "dp",
                    [(i, (i + shift) % dp_count) for i in range(dp_count)],
                )
                for array in (grad_owned[0], grad_replica[0])
            ]
        )
    sums = [part.astype(jnp.float32) for part in own_block]
    for got in received:
        sums = [total + part.astype(jnp.float32) for total, part in zip(sums, got)]
    grads = jnp.concatenate(sums, axis=0)
    source_index = jnp.sum(
        jnp.where(
            new_experts[:, None] == old_experts[None, :], lax.iota(jnp.int32, experts)[None, :], 0
        ),
        axis=1,
    )
    state_new = jnp.take(state_p, source_index, axis=1)

    grads_p = lax.all_to_all(
        grads.reshape(exp_dev + rep_dev, ep_count, piece_rows, columns).transpose(1, 0, 2, 3),
        "ep",
        split_axis=0,
        concat_axis=0,
        tiled=True,
    )
    grads_p = grads_p.reshape(ep_count * (exp_dev + rep_dev), piece_rows * columns)

    column = lax.iota(jnp.int32, ep_count * (exp_dev + rep_dev))
    device_of, within = column // (exp_dev + rep_dev), column % (exp_dev + rep_dev)
    is_owned = within < exp_dev
    old_slot = jnp.clip(device_of * exp_dev + within, 0, experts - 1)
    rep_slot = jnp.clip(device_of * rep_dev + within - exp_dev, 0, replica_slots - 1)
    live = (rep_slot % rep_dev < rep_count[rep_slot // rep_dev]).astype(jnp.float32)
    column_expert = jnp.where(is_owned, old_experts[old_slot], rep_expert[rep_slot])
    column_weight = jnp.where(is_owned, jnp.float32(1.0), live)
    combine = jnp.where(
        new_experts[:, None] == column_expert[None, :], column_weight[None, :], jnp.float32(0.0)
    )
    gradient = jnp.dot(
        combine,
        grads_p,
        precision=lax.Precision.HIGHEST,
        preferred_element_type=jnp.float32,
    ).reshape(experts, piece_rows, columns)
    moved = jnp.stack(adam_update(state_new[0], state_new[1], state_new[2], gradient))
    back = lax.all_to_all(
        moved.reshape(3, ep_count, exp_dev, piece_rows, columns).transpose(1, 0, 2, 3, 4),
        "ep",
        split_axis=0,
        concat_axis=0,
        tiled=True,
    )
    back = back.transpose(1, 2, 0, 3, 4).reshape(3, exp_dev, shard_rows, columns)
    return (back[0], back[1], back[2])


def solution(mesh):
    in_specs = (
        P("ep", "dp", None),
        P("ep", "dp", None),
        P("ep", "dp", None),
        P("dp", "ep", None, None),
        P("dp", "ep", None, None),
        P(),
        P(),
        P(),
        P(),
    )
    out_specs = (P("ep", "dp", None), P("ep", "dp", None), P("ep", "dp", None))
    return jax.shard_map(
        per_device_body, mesh=mesh, in_specs=in_specs, out_specs=out_specs, check_vma=False
    )
```

```python
import jax
import jax.numpy as jnp
from jax import lax
from jax.experimental import pallas as pl
from jax.experimental.pallas import tpu as pltpu
from jax.sharding import PartitionSpec as P

beta_first = 0.9
beta_second = 0.95
learn_rate = 0.01
decay_rate = 0.1
adam_eps = 1e-08
corr_first = 1.0 - 0.9**10
corr_second = 1.0 - 0.95**10


def adam_update(weight_now, first_now, second_now, gradient):
    moved_first = beta_first * first_now + (1.0 - beta_first) * gradient
    moved_second = beta_second * second_now + (1.0 - beta_second) * gradient * gradient
    step_size = moved_first / corr_first / (jnp.sqrt(moved_second / corr_second) + adam_eps)
    moved_weight = weight_now - learn_rate * (step_size + decay_rate * weight_now)
    return (moved_weight, moved_first, moved_second)


def exchange_kernel(src_ref, dst_ref, sems):
    count = src_ref.shape[0]
    me = lax.axis_index("ep")
    row = lax.axis_index("dp")
    mesh_id = pl.DeviceIdType.MESH

    barrier = pltpu.get_barrier_semaphore()

    def greet(k, carry):
        peer = lax.rem(me + k, count)
        pl.semaphore_signal(barrier, inc=1, device_id=(peer, row), device_id_type=mesh_id)
        return carry

    lax.fori_loop(1, count, greet, 0)
    pl.semaphore_wait(barrier, count - 1)

    local = pltpu.make_async_copy(src_ref.at[me], dst_ref.at[me], sems.at[2])
    local.start()

    def send(k, carry):
        peer = lax.rem(me + k, count)
        pltpu.make_async_remote_copy(
            src_ref=src_ref.at[peer],
            dst_ref=dst_ref.at[me],
            send_sem=sems.at[0],
            recv_sem=sems.at[1],
            device_id=(peer, row),
            device_id_type=mesh_id,
        ).start()
        return carry

    lax.fori_loop(1, count, send, 0)
    every = pltpu.make_async_remote_copy(
        src_ref=src_ref.at[pl.ds(0, count - 1)],
        dst_ref=dst_ref.at[pl.ds(0, count - 1)],
        send_sem=sems.at[0],
        recv_sem=sems.at[1],
        device_id=(lax.rem(me + 1, count), row),
        device_id_type=mesh_id,
    )
    every.wait_send()
    every.wait_recv()
    local.wait()


def exchange(array):
    size = array.size * array.dtype.itemsize
    return pl.pallas_call(
        exchange_kernel,
        out_shape=jax.ShapeDtypeStruct(array.shape, array.dtype),
        in_specs=[pl.BlockSpec(memory_space=pl.ANY)],
        out_specs=pl.BlockSpec(memory_space=pl.ANY),
        scratch_shapes=[pltpu.SemaphoreType.DMA((3,))],
        compiler_params=pltpu.CompilerParams(collective_id=0, has_side_effects=True),
        cost_estimate=pl.CostEstimate(flops=0, transcendentals=0, bytes_accessed=2 * size),
    )(array)


def per_device_body(
    master_weight,
    first_moment,
    second_moment,
    grad_owned,
    grad_replica,
    old_experts,
    new_experts,
    rep_expert,
    rep_count,
):
    ep_count = lax.axis_size("ep")
    exp_dev, shard_rows, columns = master_weight.shape
    rep_dev = grad_replica.shape[1]
    piece_rows = shard_rows // ep_count
    experts = exp_dev * ep_count
    replica_slots = rep_dev * ep_count

    state = jnp.stack([master_weight, first_moment, second_moment]).reshape(
        3, exp_dev, ep_count, piece_rows, columns
    )
    state_p = lax.all_to_all(
        state.transpose(2, 0, 1, 3, 4), "ep", split_axis=0, concat_axis=0, tiled=True
    )
    state_p = state_p.transpose(1, 0, 2, 3, 4).reshape(3, experts, piece_rows, columns)

    dp_count = lax.axis_size("dp")
    dp_index = lax.axis_index("dp")

    def block_of(array, index):
        return lax.dynamic_slice_in_dim(array, index * shard_rows, shard_rows, axis=1)

    own_block = [block_of(grad_owned[0], dp_index), block_of(grad_replica[0], dp_index)]
    received = []
    for shift in range(1, dp_count):
        target = (dp_index + shift) % dp_count
        received.append(
            [
                lax.ppermute(
                    block_of(array, target),
                    "dp",
                    [(i, (i + shift) % dp_count) for i in range(dp_count)],
                )
                for array in (grad_owned[0], grad_replica[0])
            ]
        )
    sums = [part.astype(jnp.float32) for part in own_block]
    for got in received:
        sums = [total + part.astype(jnp.float32) for total, part in zip(sums, got)]
    grads = jnp.concatenate(sums, axis=0)
    source_index = jnp.sum(
        jnp.where(
            new_experts[:, None] == old_experts[None, :], lax.iota(jnp.int32, experts)[None, :], 0
        ),
        axis=1,
    )
    state_new = jnp.take(state_p, source_index, axis=1)

    grads_p = lax.all_to_all(
        grads.reshape(exp_dev + rep_dev, ep_count, piece_rows, columns).transpose(1, 0, 2, 3),
        "ep",
        split_axis=0,
        concat_axis=0,
        tiled=True,
    )
    grads_p = grads_p.reshape(ep_count * (exp_dev + rep_dev), piece_rows * columns)

    column = lax.iota(jnp.int32, ep_count * (exp_dev + rep_dev))
    device_of, within = column // (exp_dev + rep_dev), column % (exp_dev + rep_dev)
    is_owned = within < exp_dev
    old_slot = jnp.clip(device_of * exp_dev + within, 0, experts - 1)
    rep_slot = jnp.clip(device_of * rep_dev + within - exp_dev, 0, replica_slots - 1)
    live = (rep_slot % rep_dev < rep_count[rep_slot // rep_dev]).astype(jnp.float32)
    column_expert = jnp.where(is_owned, old_experts[old_slot], rep_expert[rep_slot])
    column_weight = jnp.where(is_owned, jnp.float32(1.0), live)
    combine = jnp.where(
        new_experts[:, None] == column_expert[None, :], column_weight[None, :], jnp.float32(0.0)
    )
    gradient = jnp.dot(
        combine,
        grads_p,
        precision=lax.Precision.HIGHEST,
        preferred_element_type=jnp.float32,
    ).reshape(experts, piece_rows, columns)
    moved = jnp.stack(adam_update(state_new[0], state_new[1], state_new[2], gradient))
    back = exchange(
        moved.reshape(3, ep_count, exp_dev, piece_rows, columns).transpose(1, 0, 2, 3, 4)
    )
    back = back.transpose(1, 2, 0, 3, 4).reshape(3, exp_dev, shard_rows, columns)
    return (back[0], back[1], back[2])


def solution(mesh):
    in_specs = (
        P("ep", "dp", None),
        P("ep", "dp", None),
        P("ep", "dp", None),
        P("dp", "ep", None, None),
        P("dp", "ep", None, None),
        P(),
        P(),
        P(),
        P(),
    )
    out_specs = (P("ep", "dp", None), P("ep", "dp", None), P("ep", "dp", None))
    return jax.shard_map(
        per_device_body, mesh=mesh, in_specs=in_specs, out_specs=out_specs, check_vma=False
    )
```

```python
import jax
import jax.numpy as jnp
from jax import lax
from jax.experimental import pallas as pl
from jax.experimental.pallas import tpu as pltpu
from jax.sharding import PartitionSpec as P

beta_first = 0.9
beta_second = 0.95
learn_rate = 0.01
decay_rate = 0.1
adam_eps = 1e-08
corr_first = 1.0 - 0.9**10
corr_second = 1.0 - 0.95**10


def adam_update(weight_now, first_now, second_now, gradient):
    moved_first = beta_first * first_now + (1.0 - beta_first) * gradient
    moved_second = beta_second * second_now + (1.0 - beta_second) * gradient * gradient
    step_size = moved_first / corr_first / (jnp.sqrt(moved_second / corr_second) + adam_eps)
    moved_weight = weight_now - learn_rate * (step_size + decay_rate * weight_now)
    return (moved_weight, moved_first, moved_second)


def exchange_kernel(*refs):
    arrays = (len(refs) - 1) // 2
    srcs, dsts, sems = refs[:arrays], refs[arrays : 2 * arrays], refs[2 * arrays]
    count = srcs[0].shape[0]
    me = lax.axis_index("ep")
    row = lax.axis_index("dp")
    mesh_id = pl.DeviceIdType.MESH

    barrier = pltpu.get_barrier_semaphore()

    def greet(k, carry):
        peer = lax.rem(me + k, count)
        pl.semaphore_signal(barrier, inc=1, device_id=(peer, row), device_id_type=mesh_id)
        return carry

    lax.fori_loop(1, count, greet, 0)
    pl.semaphore_wait(barrier, count - 1)

    locals_ = []
    for a in range(arrays):
        local = pltpu.make_async_copy(srcs[a].at[me], dsts[a].at[me], sems.at[a, 2])
        local.start()
        locals_.append(local)

    def send(k, carry):
        peer = lax.rem(me + k, count)
        for a in range(arrays):
            pltpu.make_async_remote_copy(
                src_ref=srcs[a].at[peer],
                dst_ref=dsts[a].at[me],
                send_sem=sems.at[a, 0],
                recv_sem=sems.at[a, 1],
                device_id=(peer, row),
                device_id_type=mesh_id,
            ).start()
        return carry

    lax.fori_loop(1, count, send, 0)
    for a in range(arrays):
        every = pltpu.make_async_remote_copy(
            src_ref=srcs[a].at[pl.ds(0, count - 1)],
            dst_ref=dsts[a].at[pl.ds(0, count - 1)],
            send_sem=sems.at[a, 0],
            recv_sem=sems.at[a, 1],
            device_id=(lax.rem(me + 1, count), row),
            device_id_type=mesh_id,
        )
        every.wait_send()
        every.wait_recv()
        locals_[a].wait()


def exchange(*arrays):
    size = sum(array.size * array.dtype.itemsize for array in arrays)
    return pl.pallas_call(
        exchange_kernel,
        out_shape=tuple(jax.ShapeDtypeStruct(array.shape, array.dtype) for array in arrays),
        in_specs=[pl.BlockSpec(memory_space=pl.ANY)] * len(arrays),
        out_specs=tuple(pl.BlockSpec(memory_space=pl.ANY) for _ in arrays),
        scratch_shapes=[pltpu.SemaphoreType.DMA((len(arrays), 3))],
        compiler_params=pltpu.CompilerParams(collective_id=0, has_side_effects=True),
        cost_estimate=pl.CostEstimate(flops=0, transcendentals=0, bytes_accessed=2 * size),
    )(*arrays)


def per_device_body(
    master_weight,
    first_moment,
    second_moment,
    grad_owned,
    grad_replica,
    old_experts,
    new_experts,
    rep_expert,
    rep_count,
):
    ep_count = lax.axis_size("ep")
    exp_dev, shard_rows, columns = master_weight.shape
    rep_dev = grad_replica.shape[1]
    piece_rows = shard_rows // ep_count
    experts = exp_dev * ep_count
    replica_slots = rep_dev * ep_count

    state = jnp.stack([master_weight, first_moment, second_moment]).reshape(
        3, exp_dev, ep_count, piece_rows, columns
    )
    state_p = lax.all_to_all(
        state.transpose(2, 0, 1, 3, 4), "ep", split_axis=0, concat_axis=0, tiled=True
    )
    state_p = state_p.transpose(1, 0, 2, 3, 4).reshape(3, experts, piece_rows, columns)

    dp_count = lax.axis_size("dp")
    dp_index = lax.axis_index("dp")

    def block_of(array, index):
        return lax.dynamic_slice_in_dim(array, index * shard_rows, shard_rows, axis=1)

    own_block = [block_of(grad_owned[0], dp_index), block_of(grad_replica[0], dp_index)]
    received = []
    for shift in range(1, dp_count):
        target = (dp_index + shift) % dp_count
        received.append(
            [
                lax.ppermute(
                    block_of(array, target),
                    "dp",
                    [(i, (i + shift) % dp_count) for i in range(dp_count)],
                )
                for array in (grad_owned[0], grad_replica[0])
            ]
        )
    sums = [part.astype(jnp.float32) for part in own_block]
    for got in received:
        sums = [total + part.astype(jnp.float32) for total, part in zip(sums, got)]
    grads = jnp.concatenate(sums, axis=0)
    source_index = jnp.sum(
        jnp.where(
            new_experts[:, None] == old_experts[None, :], lax.iota(jnp.int32, experts)[None, :], 0
        ),
        axis=1,
    )
    state_new = jnp.take(state_p, source_index, axis=1)

    grads_p = lax.all_to_all(
        grads.reshape(exp_dev + rep_dev, ep_count, piece_rows, columns).transpose(1, 0, 2, 3),
        "ep",
        split_axis=0,
        concat_axis=0,
        tiled=True,
    )
    grads_p = grads_p.reshape(ep_count * (exp_dev + rep_dev), piece_rows * columns)

    column = lax.iota(jnp.int32, ep_count * (exp_dev + rep_dev))
    device_of, within = column // (exp_dev + rep_dev), column % (exp_dev + rep_dev)
    is_owned = within < exp_dev
    old_slot = jnp.clip(device_of * exp_dev + within, 0, experts - 1)
    rep_slot = jnp.clip(device_of * rep_dev + within - exp_dev, 0, replica_slots - 1)
    live = (rep_slot % rep_dev < rep_count[rep_slot // rep_dev]).astype(jnp.float32)
    column_expert = jnp.where(is_owned, old_experts[old_slot], rep_expert[rep_slot])
    column_weight = jnp.where(is_owned, jnp.float32(1.0), live)
    combine = jnp.where(
        new_experts[:, None] == column_expert[None, :], column_weight[None, :], jnp.float32(0.0)
    )
    gradient = jnp.dot(
        combine,
        grads_p,
        precision=lax.Precision.HIGHEST,
        preferred_element_type=jnp.float32,
    ).reshape(experts, piece_rows, columns)
    moved = adam_update(state_new[0], state_new[1], state_new[2], gradient)
    back = exchange(*(array.reshape(ep_count, exp_dev, piece_rows, columns) for array in moved))
    return tuple(
        array.transpose(1, 0, 2, 3).reshape(exp_dev, shard_rows, columns) for array in back
    )


def solution(mesh):
    in_specs = (
        P("ep", "dp", None),
        P("ep", "dp", None),
        P("ep", "dp", None),
        P("dp", "ep", None, None),
        P("dp", "ep", None, None),
        P(),
        P(),
        P(),
        P(),
    )
    out_specs = (P("ep", "dp", None), P("ep", "dp", None), P("ep", "dp", None))
    return jax.shard_map(
        per_device_body, mesh=mesh, in_specs=in_specs, out_specs=out_specs, check_vma=False
    )
```

```python
import jax
import jax.numpy as jnp
from jax import lax
from jax.experimental import pallas as pl
from jax.experimental.pallas import tpu as pltpu
from jax.sharding import PartitionSpec as P

beta_first = 0.9
beta_second = 0.95
learn_rate = 0.01
decay_rate = 0.1
adam_eps = 1e-08
corr_first = 1.0 - 0.9**10
corr_second = 1.0 - 0.95**10


def adam_update(weight_now, first_now, second_now, gradient):
    moved_first = beta_first * first_now + (1.0 - beta_first) * gradient
    moved_second = beta_second * second_now + (1.0 - beta_second) * gradient * gradient
    step_size = moved_first / corr_first / (jnp.sqrt(moved_second / corr_second) + adam_eps)
    moved_weight = weight_now - learn_rate * (step_size + decay_rate * weight_now)
    return (moved_weight, moved_first, moved_second)


def exchange_kernel(*refs):
    arrays = (len(refs) - 1) // 2
    srcs, dsts, sems = refs[:arrays], refs[arrays : 2 * arrays], refs[2 * arrays]
    count = srcs[0].shape[0]
    piece = dsts[0].shape[1] // count
    me = lax.axis_index("ep")
    row = lax.axis_index("dp")
    mesh_id = pl.DeviceIdType.MESH

    def window(ref, source):
        return ref.at[:, pl.ds(source * piece, piece), :]

    def copy(a, k, peer):
        return pltpu.make_async_remote_copy(
            src_ref=srcs[a].at[peer],
            dst_ref=window(dsts[a], me),
            send_sem=sems.at[a, 0, k],
            recv_sem=sems.at[a, 1, k],
            device_id=(peer, row),
            device_id_type=mesh_id,
        )

    barrier = pltpu.get_barrier_semaphore()

    def greet(k, carry):
        peer = lax.rem(me + k, count)
        pl.semaphore_signal(barrier, inc=1, device_id=(peer, row), device_id_type=mesh_id)
        return carry

    lax.fori_loop(1, count, greet, 0)
    pl.semaphore_wait(barrier, count - 1)

    locals_ = []
    for a in range(arrays):
        local = pltpu.make_async_copy(srcs[a].at[me], window(dsts[a], me), sems.at[a, 0, 0])
        local.start()
        locals_.append(local)

    def send(k, carry):
        peer = lax.rem(me + k, count)
        for a in range(arrays):
            copy(a, k, peer).start()
        return carry

    lax.fori_loop(1, count, send, 0)

    def finish(k, carry):
        peer = lax.rem(me + k, count)
        for a in range(arrays):
            copy(a, k, peer).wait_send()
            pltpu.make_async_remote_copy(
                src_ref=srcs[a].at[peer],
                dst_ref=window(dsts[a], lax.rem(me + count - k, count)),
                send_sem=sems.at[a, 0, k],
                recv_sem=sems.at[a, 1, k],
                device_id=(peer, row),
                device_id_type=mesh_id,
            ).wait_recv()
        return carry

    lax.fori_loop(1, count, finish, 0)
    for local in locals_:
        local.wait()


def exchange(rows, *arrays):
    count, slots, _, lanes = arrays[0].shape
    size = sum(array.size * array.dtype.itemsize for array in arrays)
    return pl.pallas_call(
        exchange_kernel,
        out_shape=tuple(
            jax.ShapeDtypeStruct((slots, rows, lanes), array.dtype) for array in arrays
        ),
        in_specs=[pl.BlockSpec(memory_space=pl.ANY)] * len(arrays),
        out_specs=tuple(pl.BlockSpec(memory_space=pl.ANY) for _ in arrays),
        scratch_shapes=[pltpu.SemaphoreType.DMA((len(arrays), 2, count))],
        compiler_params=pltpu.CompilerParams(collective_id=0, has_side_effects=True),
        cost_estimate=pl.CostEstimate(flops=0, transcendentals=0, bytes_accessed=2 * size),
    )(*arrays)


def per_device_body(
    master_weight,
    first_moment,
    second_moment,
    grad_owned,
    grad_replica,
    old_experts,
    new_experts,
    rep_expert,
    rep_count,
):
    ep_count = lax.axis_size("ep")
    exp_dev, shard_rows, columns = master_weight.shape
    rep_dev = grad_replica.shape[1]
    piece_rows = shard_rows // ep_count
    experts = exp_dev * ep_count
    replica_slots = rep_dev * ep_count

    state = jnp.stack([master_weight, first_moment, second_moment]).reshape(
        3, exp_dev, ep_count, piece_rows, columns
    )
    state_p = lax.all_to_all(
        state.transpose(2, 0, 1, 3, 4), "ep", split_axis=0, concat_axis=0, tiled=True
    )
    state_p = state_p.transpose(1, 0, 2, 3, 4).reshape(3, experts, piece_rows, columns)

    dp_count = lax.axis_size("dp")
    dp_index = lax.axis_index("dp")

    def block_of(array, index):
        return lax.dynamic_slice_in_dim(array, index * shard_rows, shard_rows, axis=1)

    own_block = [block_of(grad_owned[0], dp_index), block_of(grad_replica[0], dp_index)]
    received = []
    for shift in range(1, dp_count):
        target = (dp_index + shift) % dp_count
        received.append(
            [
                lax.ppermute(
                    block_of(array, target),
                    "dp",
                    [(i, (i + shift) % dp_count) for i in range(dp_count)],
                )
                for array in (grad_owned[0], grad_replica[0])
            ]
        )
    sums = [part.astype(jnp.float32) for part in own_block]
    for got in received:
        sums = [total + part.astype(jnp.float32) for total, part in zip(sums, got)]
    grads = jnp.concatenate(sums, axis=0)
    source_index = jnp.sum(
        jnp.where(
            new_experts[:, None] == old_experts[None, :], lax.iota(jnp.int32, experts)[None, :], 0
        ),
        axis=1,
    )
    state_new = jnp.take(state_p, source_index, axis=1)

    grads_p = lax.all_to_all(
        grads.reshape(exp_dev + rep_dev, ep_count, piece_rows, columns).transpose(1, 0, 2, 3),
        "ep",
        split_axis=0,
        concat_axis=0,
        tiled=True,
    )
    grads_p = grads_p.reshape(ep_count * (exp_dev + rep_dev), piece_rows * columns)

    column = lax.iota(jnp.int32, ep_count * (exp_dev + rep_dev))
    device_of, within = column // (exp_dev + rep_dev), column % (exp_dev + rep_dev)
    is_owned = within < exp_dev
    old_slot = jnp.clip(device_of * exp_dev + within, 0, experts - 1)
    rep_slot = jnp.clip(device_of * rep_dev + within - exp_dev, 0, replica_slots - 1)
    live = (rep_slot % rep_dev < rep_count[rep_slot // rep_dev]).astype(jnp.float32)
    column_expert = jnp.where(is_owned, old_experts[old_slot], rep_expert[rep_slot])
    column_weight = jnp.where(is_owned, jnp.float32(1.0), live)
    combine = jnp.where(
        new_experts[:, None] == column_expert[None, :], column_weight[None, :], jnp.float32(0.0)
    )
    gradient = jnp.dot(
        combine,
        grads_p,
        precision=lax.Precision.HIGHEST,
        preferred_element_type=jnp.float32,
    ).reshape(experts, piece_rows, columns)
    moved = adam_update(state_new[0], state_new[1], state_new[2], gradient)
    return exchange(
        shard_rows, *(array.reshape(ep_count, exp_dev, piece_rows, columns) for array in moved)
    )


def solution(mesh):
    in_specs = (
        P("ep", "dp", None),
        P("ep", "dp", None),
        P("ep", "dp", None),
        P("dp", "ep", None, None),
        P("dp", "ep", None, None),
        P(),
        P(),
        P(),
        P(),
    )
    out_specs = (P("ep", "dp", None), P("ep", "dp", None), P("ep", "dp", None))
    return jax.shard_map(
        per_device_body, mesh=mesh, in_specs=in_specs, out_specs=out_specs, check_vma=False
    )
```

```python
import jax
import jax.numpy as jnp
from jax import lax
from jax.experimental import pallas as pl
from jax.experimental.pallas import tpu as pltpu
from jax.sharding import PartitionSpec as P

beta_first = 0.9
beta_second = 0.95
learn_rate = 0.01
decay_rate = 0.1
adam_eps = 1e-08
corr_first = 1.0 - 0.9**10
corr_second = 1.0 - 0.95**10


def adam_update(weight_now, first_now, second_now, gradient):
    moved_first = beta_first * first_now + (1.0 - beta_first) * gradient
    moved_second = beta_second * second_now + (1.0 - beta_second) * gradient * gradient
    step_size = moved_first / corr_first / (jnp.sqrt(moved_second / corr_second) + adam_eps)
    moved_weight = weight_now - learn_rate * (step_size + decay_rate * weight_now)
    return (moved_weight, moved_first, moved_second)


def spread_kernel(w, f, s, go, gr, sw, sf, ss, ro, rr, ep_sems, dp_sems, own_sems):
    states, pieces, grads, blocks = (w, f, s), (sw, sf, ss), (go, gr), (ro, rr)
    count = lax.axis_size("ep")
    dp_count = lax.axis_size("dp")
    exp_dev = w.shape[0]
    piece = w.shape[1] // count
    rows = w.shape[1]
    me = lax.axis_index("ep")
    row = lax.axis_index("dp")
    mesh_id = pl.DeviceIdType.MESH

    def window(ref, owner):
        return ref.at[:, pl.ds(owner * piece, piece), :]

    def slots(ref, source):
        return ref.at[pl.ds(source * exp_dev, exp_dev)]

    def band(ref, target):
        return ref.at[:, pl.ds(target * rows, rows), :]

    barrier = pltpu.get_barrier_semaphore()

    def greet(k, carry):
        pl.semaphore_signal(
            barrier, inc=1, device_id=(lax.rem(me + k, count), row), device_id_type=mesh_id
        )
        return carry

    lax.fori_loop(1, count, greet, 0)
    for shift in range(1, dp_count):
        pl.semaphore_signal(
            barrier, inc=1, device_id=(me, (row + shift) % dp_count), device_id_type=mesh_id
        )
    pl.semaphore_wait(barrier, count - 1 + dp_count - 1)

    def dp_copy(b, shift, send_target):
        return pltpu.make_async_remote_copy(
            src_ref=band(grads[b], send_target),
            dst_ref=blocks[b].at[shift - 1],
            send_sem=dp_sems.at[b, 0, shift],
            recv_sem=dp_sems.at[b, 1, shift],
            device_id=(me, send_target),
            device_id_type=mesh_id,
        )

    local = []
    for a in range(3):
        copy = pltpu.make_async_copy(window(states[a], me), slots(pieces[a], me), own_sems.at[a])
        copy.start()
        local.append(copy)

    def ep_copy(a, k, peer, source):
        return pltpu.make_async_remote_copy(
            src_ref=window(states[a], peer),
            dst_ref=slots(pieces[a], source),
            send_sem=ep_sems.at[a, 0, k],
            recv_sem=ep_sems.at[a, 1, k],
            device_id=(peer, row),
            device_id_type=mesh_id,
        )

    def send(k, carry):
        peer = lax.rem(me + k, count)
        for a in range(3):
            ep_copy(a, k, peer, me).start()
        return carry

    lax.fori_loop(1, count, send, 0)
    for shift in range(1, dp_count):
        for b in range(2):
            dp_copy(b, shift, (row + shift) % dp_count).start()

    def finish(k, carry):
        peer = lax.rem(me + k, count)
        source = lax.rem(me + count - k, count)
        for a in range(3):
            ep_copy(a, k, peer, me).wait_send()
            ep_copy(a, k, peer, source).wait_recv()
        return carry

    lax.fori_loop(1, count, finish, 0)
    for shift in range(1, dp_count):
        for b in range(2):
            copy = dp_copy(b, shift, (row + shift) % dp_count)
            copy.wait_send()
            copy.wait_recv()
    for copy in local:
        copy.wait()


def spread(w, f, s, go, gr):
    count, dp_count = 64, 4
    exp_dev, rows, lanes = w.shape
    piece = rows // count
    state_out = jax.ShapeDtypeStruct((exp_dev * count, piece, lanes), w.dtype)
    grad_out = jax.ShapeDtypeStruct((dp_count - 1, go.shape[0], rows, lanes), go.dtype)
    size = 3 * w.size * w.dtype.itemsize + 2 * go.size * go.dtype.itemsize
    return pl.pallas_call(
        spread_kernel,
        out_shape=(state_out, state_out, state_out, grad_out, grad_out),
        in_specs=[pl.BlockSpec(memory_space=pl.ANY)] * 5,
        out_specs=tuple(pl.BlockSpec(memory_space=pl.ANY) for _ in range(5)),
        scratch_shapes=[
            pltpu.SemaphoreType.DMA((3, 2, count)),
            pltpu.SemaphoreType.DMA((2, 2, dp_count)),
            pltpu.SemaphoreType.DMA((3,)),
        ],
        compiler_params=pltpu.CompilerParams(collective_id=0, has_side_effects=True),
        cost_estimate=pl.CostEstimate(flops=0, transcendentals=0, bytes_accessed=2 * size),
    )(w, f, s, go, gr)


def per_device_body(
    master_weight,
    first_moment,
    second_moment,
    grad_owned,
    grad_replica,
    old_experts,
    new_experts,
    rep_expert,
    rep_count,
):
    ep_count = lax.axis_size("ep")
    exp_dev, shard_rows, columns = master_weight.shape
    rep_dev = grad_replica.shape[1]
    piece_rows = shard_rows // ep_count
    experts = exp_dev * ep_count
    replica_slots = rep_dev * ep_count

    dp_count = lax.axis_size("dp")
    dp_index = lax.axis_index("dp")
    sw, sf, ss, ro, rr = spread(
        master_weight, first_moment, second_moment, grad_owned[0], grad_replica[0]
    )

    def block_of(array, index):
        return lax.dynamic_slice_in_dim(array, index * shard_rows, shard_rows, axis=1)

    own_block = [block_of(grad_owned[0], dp_index), block_of(grad_replica[0], dp_index)]
    received = [[ro[i], rr[i]] for i in range(dp_count - 1)]
    sums = [part.astype(jnp.float32) for part in own_block]
    for got in received:
        sums = [total + part.astype(jnp.float32) for total, part in zip(sums, got)]
    grads = jnp.concatenate(sums, axis=0)
    source_index = jnp.sum(
        jnp.where(
            new_experts[:, None] == old_experts[None, :], lax.iota(jnp.int32, experts)[None, :], 0
        ),
        axis=1,
    )
    state_new = [jnp.take(x, source_index, axis=0) for x in (sw, sf, ss)]

    grads_p = lax.all_to_all(
        grads.reshape(exp_dev + rep_dev, ep_count, piece_rows, columns).transpose(1, 0, 2, 3),
        "ep",
        split_axis=0,
        concat_axis=0,
        tiled=True,
    )
    grads_p = grads_p.reshape(ep_count * (exp_dev + rep_dev), piece_rows * columns)

    column = lax.iota(jnp.int32, ep_count * (exp_dev + rep_dev))
    device_of, within = column // (exp_dev + rep_dev), column % (exp_dev + rep_dev)
    is_owned = within < exp_dev
    old_slot = jnp.clip(device_of * exp_dev + within, 0, experts - 1)
    rep_slot = jnp.clip(device_of * rep_dev + within - exp_dev, 0, replica_slots - 1)
    live = (rep_slot % rep_dev < rep_count[rep_slot // rep_dev]).astype(jnp.float32)
    column_expert = jnp.where(is_owned, old_experts[old_slot], rep_expert[rep_slot])
    column_weight = jnp.where(is_owned, jnp.float32(1.0), live)
    combine = jnp.where(
        new_experts[:, None] == column_expert[None, :], column_weight[None, :], jnp.float32(0.0)
    )
    gradient = jnp.dot(
        combine,
        grads_p,
        precision=lax.Precision.HIGHEST,
        preferred_element_type=jnp.float32,
    ).reshape(experts, piece_rows, columns)
    moved = jnp.stack(adam_update(state_new[0], state_new[1], state_new[2], gradient))
    back = lax.all_to_all(
        moved.reshape(3, ep_count, exp_dev, piece_rows, columns).transpose(1, 0, 2, 3, 4),
        "ep",
        split_axis=0,
        concat_axis=0,
        tiled=True,
    )
    back = back.transpose(1, 2, 0, 3, 4).reshape(3, exp_dev, shard_rows, columns)
    return (back[0], back[1], back[2])


def solution(mesh):
    in_specs = (
        P("ep", "dp", None),
        P("ep", "dp", None),
        P("ep", "dp", None),
        P("dp", "ep", None, None),
        P("dp", "ep", None, None),
        P(),
        P(),
        P(),
        P(),
    )
    out_specs = (P("ep", "dp", None), P("ep", "dp", None), P("ep", "dp", None))
    return jax.shard_map(
        per_device_body, mesh=mesh, in_specs=in_specs, out_specs=out_specs, check_vma=False
    )
```

```python
import jax
import jax.numpy as jnp
from jax import lax
from jax.sharding import PartitionSpec as P

beta_first = 0.9
beta_second = 0.95
learn_rate = 0.01
decay_rate = 0.1
adam_eps = 1e-08
corr_first = 1.0 - 0.9**10
corr_second = 1.0 - 0.95**10


def per_device_body(
    master_weight,
    first_moment,
    second_moment,
    grad_owned,
    grad_replica,
    old_experts,
    new_experts,
    rep_expert,
    rep_count,
):
    ep_count = lax.axis_size("ep")
    exp_dev, shard_rows, columns = master_weight.shape
    rep_dev = grad_replica.shape[1]
    piece_rows = shard_rows // ep_count
    experts = exp_dev * ep_count
    replica_slots = rep_dev * ep_count

    state = jnp.stack([master_weight, first_moment, second_moment]).reshape(
        3, exp_dev, ep_count, piece_rows, columns
    )
    state_p = lax.all_to_all(
        state.transpose(2, 0, 1, 3, 4), "ep", split_axis=0, concat_axis=0, tiled=True
    )
    state_p = state_p.transpose(1, 0, 2, 3, 4).reshape(3, experts, piece_rows, columns)

    dp_count = lax.axis_size("dp")
    dp_index = lax.axis_index("dp")

    def block_of(array, index):
        return lax.dynamic_slice_in_dim(array, index * shard_rows, shard_rows, axis=1)

    own_block = [block_of(grad_owned[0], dp_index), block_of(grad_replica[0], dp_index)]
    received = []
    for shift in range(1, dp_count):
        target = (dp_index + shift) % dp_count
        received.append(
            [
                lax.ppermute(
                    block_of(array, target),
                    "dp",
                    [(i, (i + shift) % dp_count) for i in range(dp_count)],
                )
                for array in (grad_owned[0], grad_replica[0])
            ]
        )
    sums = [part.astype(jnp.float32) for part in own_block]
    for got in received:
        sums = [total + part.astype(jnp.float32) for total, part in zip(sums, got)]
    grads = jnp.concatenate(sums, axis=0)
    source_index = jnp.sum(
        jnp.where(
            new_experts[:, None] == old_experts[None, :], lax.iota(jnp.int32, experts)[None, :], 0
        ),
        axis=1,
    )
    state_new = jnp.take(state_p, source_index, axis=1)

    grads_p = lax.all_to_all(
        grads.reshape(exp_dev + rep_dev, ep_count, piece_rows, columns).transpose(1, 0, 2, 3),
        "ep",
        split_axis=0,
        concat_axis=0,
        tiled=True,
    )
    grads_p = grads_p.reshape(ep_count * (exp_dev + rep_dev), piece_rows * columns)

    column = lax.iota(jnp.int32, ep_count * (exp_dev + rep_dev))
    device_of, within = column // (exp_dev + rep_dev), column % (exp_dev + rep_dev)
    is_owned = within < exp_dev
    old_slot = jnp.clip(device_of * exp_dev + within, 0, experts - 1)
    rep_slot = jnp.clip(device_of * rep_dev + within - exp_dev, 0, replica_slots - 1)
    live = (rep_slot % rep_dev < rep_count[rep_slot // rep_dev]).astype(jnp.float32)
    column_expert = jnp.where(is_owned, old_experts[old_slot], rep_expert[rep_slot])
    column_weight = jnp.where(is_owned, jnp.float32(1.0), live)
    combine = jnp.where(
        new_experts[:, None] == column_expert[None, :], column_weight[None, :], jnp.float32(0.0)
    )
    gradient = jnp.dot(
        combine,
        grads_p,
        precision=lax.Precision.HIGHEST,
        preferred_element_type=jnp.float32,
    ).reshape(experts, piece_rows, columns)
    weight_now, first_now, second_now = state_new
    moved_first = beta_first * first_now + (1.0 - beta_first) * gradient
    moved_second = beta_second * second_now + (1.0 - beta_second) * gradient * gradient

    def send_home(parts):
        count = parts.shape[0]
        back = lax.all_to_all(
            parts.reshape(count, ep_count, exp_dev, piece_rows, columns).transpose(1, 0, 2, 3, 4),
            "ep",
            split_axis=0,
            concat_axis=0,
            tiled=True,
        )
        return back.transpose(1, 2, 0, 3, 4).reshape(count, exp_dev, shard_rows, columns)

    moments = send_home(jnp.stack([moved_first, moved_second]))
    step_size = moved_first / corr_first / (jnp.sqrt(moved_second / corr_second) + adam_eps)
    moved_weight = weight_now - learn_rate * (step_size + decay_rate * weight_now)
    weight = send_home(moved_weight[None])
    return (weight[0], moments[0], moments[1])


def solution(mesh):
    in_specs = (
        P("ep", "dp", None),
        P("ep", "dp", None),
        P("ep", "dp", None),
        P("dp", "ep", None, None),
        P("dp", "ep", None, None),
        P(),
        P(),
        P(),
        P(),
    )
    out_specs = (P("ep", "dp", None), P("ep", "dp", None), P("ep", "dp", None))
    return jax.shard_map(
        per_device_body, mesh=mesh, in_specs=in_specs, out_specs=out_specs, check_vma=False
    )
```

```python
import jax
import jax.numpy as jnp
from jax import lax
from jax.experimental import pallas as pl
from jax.experimental.pallas import tpu as pltpu
from jax.sharding import PartitionSpec as P

beta_first = 0.9
beta_second = 0.95
learn_rate = 0.01
decay_rate = 0.1
adam_eps = 1e-08
corr_first = 1.0 - 0.9**10
corr_second = 1.0 - 0.95**10


def adam_update(weight_now, first_now, second_now, gradient):
    moved_first = beta_first * first_now + (1.0 - beta_first) * gradient
    moved_second = beta_second * second_now + (1.0 - beta_second) * gradient * gradient
    step_size = moved_first / corr_first / (jnp.sqrt(moved_second / corr_second) + adam_eps)
    moved_weight = weight_now - learn_rate * (step_size + decay_rate * weight_now)
    return (moved_weight, moved_first, moved_second)


def spread_kernel(w, f, s, go, gr, sw, sf, ss, ro, rr, ep_sems, dp_sems, own_sems):
    states, pieces, grads, blocks = (w, f, s), (sw, sf, ss), (go, gr), (ro, rr)
    count = lax.axis_size("ep")
    dp_count = lax.axis_size("dp")
    exp_dev = w.shape[0]
    piece = w.shape[1] // count
    rows = w.shape[1]
    me = lax.axis_index("ep")
    row = lax.axis_index("dp")
    mesh_id = pl.DeviceIdType.MESH

    def window(ref, owner):
        return ref.at[:, pl.ds(owner * piece, piece), :]

    def slots(ref, source):
        return ref.at[pl.ds(source * exp_dev, exp_dev)]

    def band(ref, target):
        return ref.at[:, pl.ds(target * rows, rows), :]

    barrier = pltpu.get_barrier_semaphore()

    def greet(k, carry):
        pl.semaphore_signal(
            barrier, inc=1, device_id=(lax.rem(me + k, count), row), device_id_type=mesh_id
        )
        return carry

    lax.fori_loop(1, count, greet, 0)
    for shift in range(1, dp_count):
        pl.semaphore_signal(
            barrier, inc=1, device_id=(me, (row + shift) % dp_count), device_id_type=mesh_id
        )
    pl.semaphore_wait(barrier, count - 1 + dp_count - 1)

    def dp_copy(b, shift, send_target):
        return pltpu.make_async_remote_copy(
            src_ref=band(grads[b], send_target),
            dst_ref=blocks[b].at[shift - 1],
            send_sem=dp_sems.at[b, 0, shift],
            recv_sem=dp_sems.at[b, 1, shift],
            device_id=(me, send_target),
            device_id_type=mesh_id,
        )

    local = []
    for a in range(3):
        copy = pltpu.make_async_copy(window(states[a], me), slots(pieces[a], me), own_sems.at[a])
        copy.start()
        local.append(copy)

    def ep_copy(a, k, peer, source):
        return pltpu.make_async_remote_copy(
            src_ref=window(states[a], peer),
            dst_ref=slots(pieces[a], source),
            send_sem=ep_sems.at[a, 0, k],
            recv_sem=ep_sems.at[a, 1, k],
            device_id=(peer, row),
            device_id_type=mesh_id,
        )

    def send(k, carry):
        peer = lax.rem(me + k, count)
        for a in range(3):
            ep_copy(a, k, peer, me).start()
        return carry

    lax.fori_loop(1, count, send, 0)
    for shift in range(1, dp_count):
        for b in range(2):
            dp_copy(b, shift, (row + shift) % dp_count).start()

    def finish(k, carry):
        peer = lax.rem(me + k, count)
        source = lax.rem(me + count - k, count)
        for a in range(3):
            ep_copy(a, k, peer, me).wait_send()
            ep_copy(a, k, peer, source).wait_recv()
        return carry

    lax.fori_loop(1, count, finish, 0)
    for shift in range(1, dp_count):
        for b in range(2):
            copy = dp_copy(b, shift, (row + shift) % dp_count)
            copy.wait_send()
            copy.wait_recv()
    for copy in local:
        copy.wait()


def spread(w, f, s, go, gr):
    count, dp_count = 64, 4
    exp_dev, rows, lanes = w.shape
    piece = rows // count
    state_out = jax.ShapeDtypeStruct((exp_dev * count, piece, lanes), w.dtype)
    grad_out = jax.ShapeDtypeStruct((dp_count - 1, go.shape[0], rows, lanes), go.dtype)
    size = 3 * w.size * w.dtype.itemsize + 2 * go.size * go.dtype.itemsize
    return pl.pallas_call(
        spread_kernel,
        out_shape=(state_out, state_out, state_out, grad_out, grad_out),
        in_specs=[pl.BlockSpec(memory_space=pltpu.VMEM)] * 3
        + [pl.BlockSpec(memory_space=pl.ANY)] * 2,
        out_specs=tuple(pl.BlockSpec(memory_space=pl.ANY) for _ in range(5)),
        scratch_shapes=[
            pltpu.SemaphoreType.DMA((3, 2, count)),
            pltpu.SemaphoreType.DMA((2, 2, dp_count)),
            pltpu.SemaphoreType.DMA((3,)),
        ],
        compiler_params=pltpu.CompilerParams(
            collective_id=0, has_side_effects=True, vmem_limit_bytes=32 * 1024 * 1024
        ),
        cost_estimate=pl.CostEstimate(flops=0, transcendentals=0, bytes_accessed=2 * size),
    )(w, f, s, go, gr)


def per_device_body(
    master_weight,
    first_moment,
    second_moment,
    grad_owned,
    grad_replica,
    old_experts,
    new_experts,
    rep_expert,
    rep_count,
):
    ep_count = lax.axis_size("ep")
    exp_dev, shard_rows, columns = master_weight.shape
    rep_dev = grad_replica.shape[1]
    piece_rows = shard_rows // ep_count
    experts = exp_dev * ep_count
    replica_slots = rep_dev * ep_count

    dp_count = lax.axis_size("dp")
    dp_index = lax.axis_index("dp")
    sw, sf, ss, ro, rr = spread(
        master_weight, first_moment, second_moment, grad_owned[0], grad_replica[0]
    )

    def block_of(array, index):
        return lax.dynamic_slice_in_dim(array, index * shard_rows, shard_rows, axis=1)

    own_block = [block_of(grad_owned[0], dp_index), block_of(grad_replica[0], dp_index)]
    received = [[ro[i], rr[i]] for i in range(dp_count - 1)]
    sums = [part.astype(jnp.float32) for part in own_block]
    for got in received:
        sums = [total + part.astype(jnp.float32) for total, part in zip(sums, got)]
    grads = jnp.concatenate(sums, axis=0)
    source_index = jnp.sum(
        jnp.where(
            new_experts[:, None] == old_experts[None, :], lax.iota(jnp.int32, experts)[None, :], 0
        ),
        axis=1,
    )
    state_new = [jnp.take(x, source_index, axis=0) for x in (sw, sf, ss)]

    grads_p = lax.all_to_all(
        grads.reshape(exp_dev + rep_dev, ep_count, piece_rows, columns).transpose(1, 0, 2, 3),
        "ep",
        split_axis=0,
        concat_axis=0,
        tiled=True,
    )
    grads_p = grads_p.reshape(ep_count * (exp_dev + rep_dev), piece_rows * columns)

    column = lax.iota(jnp.int32, ep_count * (exp_dev + rep_dev))
    device_of, within = column // (exp_dev + rep_dev), column % (exp_dev + rep_dev)
    is_owned = within < exp_dev
    old_slot = jnp.clip(device_of * exp_dev + within, 0, experts - 1)
    rep_slot = jnp.clip(device_of * rep_dev + within - exp_dev, 0, replica_slots - 1)
    live = (rep_slot % rep_dev < rep_count[rep_slot // rep_dev]).astype(jnp.float32)
    column_expert = jnp.where(is_owned, old_experts[old_slot], rep_expert[rep_slot])
    column_weight = jnp.where(is_owned, jnp.float32(1.0), live)
    combine = jnp.where(
        new_experts[:, None] == column_expert[None, :], column_weight[None, :], jnp.float32(0.0)
    )
    gradient = jnp.dot(
        combine,
        grads_p,
        precision=lax.Precision.HIGHEST,
        preferred_element_type=jnp.float32,
    ).reshape(experts, piece_rows, columns)
    moved = jnp.stack(adam_update(state_new[0], state_new[1], state_new[2], gradient))
    back = lax.all_to_all(
        moved.reshape(3, ep_count, exp_dev, piece_rows, columns).transpose(1, 0, 2, 3, 4),
        "ep",
        split_axis=0,
        concat_axis=0,
        tiled=True,
    )
    back = back.transpose(1, 2, 0, 3, 4).reshape(3, exp_dev, shard_rows, columns)
    return (back[0], back[1], back[2])


def solution(mesh):
    in_specs = (
        P("ep", "dp", None),
        P("ep", "dp", None),
        P("ep", "dp", None),
        P("dp", "ep", None, None),
        P("dp", "ep", None, None),
        P(),
        P(),
        P(),
        P(),
    )
    out_specs = (P("ep", "dp", None), P("ep", "dp", None), P("ep", "dp", None))
    return jax.shard_map(
        per_device_body, mesh=mesh, in_specs=in_specs, out_specs=out_specs, check_vma=False
    )
```
